32 devices in a mesh: group: 2 (over y), gene: 4 (over z), lat: 2 (over x), sub: 2 (over core).
Axes of the slice: x: 2, y: 2, z: 4, core: 2. Of those that a mesh axis runs over, the one named last changes fastest.
Arguments:
- cell_index: int32 [2048], P(('group', 'lat', 'sub')), parts along dimension 0, may hold values from 0 to 511
- coords_table: float32 [4, 2048], P('group', ('lat', 'sub')), parts along dimension 0, may hold values from 0 to 1
- expr_table: bfloat16 [4096, 16384], P(('group', 'lat', 'sub'), 'gene'), parts along dimension 0, may hold values from -6 to 6
- inducing: float32 [4, 64, 8192], P('group', 'lat', 'sub'), parts along dimension 0, may hold values from 0 to 1
- ind_weights: float32 [128, 8192], P(('group', 'lat'), 'sub'), parts along dimension 0, may hold values from -0.6 to 0.6
- lengthscale: float32 [128], P(('group', 'lat')), parts along dimension 0, may hold values from 0.02 to 0.1
- variance: float32 [128], P(('group', 'lat')), parts along dimension 0, may hold values from 0.5 to 2
- mixing: bfloat16 [128, 16384], P('group', 'gene'), parts along dimension 0, may hold values from -0.75 to 0.75
- noise_prec: float32 [32768], P(('group', 'gene')), parts along dimension 0, may hold values from 0.5 to 4
Outputs:
- grad_mixing: float32 [128, 16384], P('group', 'gene'), parts along dimension 0
- grad_inducing: float32 [128, 8192], P(('group', 'lat'), 'sub'), parts along dimension 0
The draws below stay inside these ranges and needn't reach their ends.
There are 2 independent parts, one for each index of `group`. The reference program is written for one: setup_inputs(seed, part) draws one part's arguments, and reference() takes and returns one part's arrays. A program takes and returns all parts, laid end to end along the dimension named above; each array names one. Nothing has to cross between parts.
Inputs may be any that keep to these rules, and one draw needn't show every extreme that they name: Entry n indexes a row inside block n // 256 of the tables: cell n is table row (n // 256) * 512 + cell_index[n]; cells may repeat.
All inputs are finite; a program needn't handle non-finite values.
Results may differ from the reference program's by a relative error of at most 0.00075.
Values may be sent and summed in bfloat16 or wider, within the bound.
A program may use at most 64 MiB of HBM per device.

```python
import math
import jax
import jax.numpy as jnp
from jax import lax

G = 16384
Q = 64
M = 8192
BAT_DEV = 256
TAB_DEV = 512
BATCH = 1024
TABLE = 2048


def plant(result, own_key, least, largest):
    place = [jax.random.randint(jax.random.fold_in(own_key, axis), (), 0, length) for axis, length in enumerate(result.shape)]
    main_axis = result.shape.index(max(result.shape))
    next_to = place[:main_axis] + [(place[main_axis] + 1) % result.shape[main_axis]] + place[main_axis + 1:]
    return result.at[tuple(place)].set(least).at[tuple(next_to)].set(largest)


def levels(own_key, extent, cuts, smallest, high):
    level = 1.0
    for position, shards_of in cuts:
        draws = jax.random.uniform(jax.random.fold_in(jax.random.fold_in(own_key, 6), position), (shards_of,), jnp.float32, smallest / len(cuts), high / len(cuts))
        level = level * jnp.repeat(jnp.exp(draws), extent[position] // shards_of).reshape((-1,) + (1,) * (len(extent) - 1 - position))
    return level


def gaussian(key, dims, width, reach, cuts=(), kind=jnp.bfloat16):
    result = jax.random.normal(key, dims, jnp.float32) * width
    if len(cuts) > 0:
        result = levels(key, dims, cuts, -0.22, 0.18) * result
    return jnp.clip(result, min=-reach, max=reach).astype(kind)


def setup_inputs(seed: int = 0, part: int = 0) -> dict:
    keys = jax.random.split(jax.random.key(seed), 10)
    own_keys = jax.random.split(jax.random.fold_in(keys[9], part), 10)
    cell_index = plant(jax.random.randint(own_keys[0], (BATCH,), 0, TAB_DEV), jax.random.fold_in(own_keys[0], 1), 0, TAB_DEV - 1).astype(jnp.int32)
    coords_table = jnp.clip(1.0 * jax.random.uniform(own_keys[1], (2, TABLE), jnp.float32) ** levels(own_keys[1], (2, TABLE), ((1, 4),), -0.2, 0.2), 0.0, 1.0)
    expr_table = gaussian(own_keys[2], (TABLE, G), 1.0, 6.0, ((0, 4), (1, 4)))
    inducing = jnp.clip(1.0 * jax.random.uniform(own_keys[3], (2, Q, M), jnp.float32) ** levels(own_keys[3], (2, Q, M), ((1, 2), (2, 2)), -0.2, 0.2), 0.0, 1.0)
    ind_weights = gaussian(own_keys[4], (Q, M), 0.1, 0.6, ((0, 2), (1, 2)), jnp.float32)
    lengthscale = jnp.clip(jnp.exp(math.log(0.1) - 1.609438 * jax.random.uniform(own_keys[5], (Q,), jnp.float32) ** levels(own_keys[5], (Q,), ((0, 2),), -0.2, 0.2)), 0.02, 0.1)
    variance = jnp.clip(jnp.exp(math.log(2.0) - 1.3862944 * jax.random.uniform(own_keys[6], (Q,), jnp.float32) ** levels(own_keys[6], (Q,), ((0, 2),), -0.2, 0.2)), 0.5, 2.0)
    mixing = gaussian(own_keys[7], (Q, G), Q ** -0.5, 0.75, ((1, 4),))
    noise_prec = jnp.clip(jnp.exp(math.log(4.0) - 2.0794415 * jax.random.uniform(own_keys[8], (G,), jnp.float32) ** levels(own_keys[8], (G,), ((0, 4),), -0.2, 0.2)), 0.5, 4.0)
    return dict(cell_index=cell_index, coords_table=coords_table, expr_table=expr_table, inducing=inducing, ind_weights=ind_weights, lengthscale=lengthscale, variance=variance, mixing=mixing, noise_prec=noise_prec)


def kernel_tile(cell_xy, points, length, height):
    delta_x = cell_xy[0][:, None] - points[0][None, :]
    delta_y = cell_xy[1][:, None] - points[1][None, :]
    return height * jnp.exp(-(delta_x * delta_x + delta_y * delta_y) * (0.5 / (length * length)))

def reference(cell_index, coords_table, expr_table, inducing, ind_weights, lengthscale, variance, mixing, noise_prec):
    cell_count = cell_index.shape[0]
    block_start = jnp.arange(cell_count, dtype=jnp.int32) // BAT_DEV * TAB_DEV
    table_rows = block_start + cell_index.astype(jnp.int32)
    cell_xy = jnp.take(coords_table, table_rows, axis=1)
    observed = jnp.take(expr_table, table_rows, axis=0)
    moved = jnp.moveaxis(inducing, 1, 0)

    def forward(packed):
        points, weights, length, height = packed
        return jnp.dot(kernel_tile(cell_xy, points, length, height), weights, precision=lax.Precision.HIGHEST)
    latent = lax.map(forward, (moved, ind_weights, lengthscale, variance)).astype(jnp.bfloat16)
    predicted = lax.dot_general(latent, mixing, (((0,), (0,)), ((), ())), preferred_element_type=jnp.float32)
    weighted = (noise_prec[None, :] * (observed.astype(jnp.float32) - predicted)).astype(jnp.bfloat16)
    grad_scale = -1.0 / math.sqrt(cell_count)
    grad_mixing = grad_scale * jnp.dot(latent, weighted, preferred_element_type=jnp.float32)
    latent_grad = grad_scale * lax.dot_general(mixing, weighted, (((1,), (1,)), ((), ())), preferred_element_type=jnp.float32)

    def backward(packed):
        points, gradient, length, height = packed
        return jnp.dot(gradient, kernel_tile(cell_xy, points, length, height), precision=lax.Precision.HIGHEST)
    grad_inducing = lax.map(backward, (moved, latent_grad, lengthscale, variance))
    return (grad_mixing, grad_inducing)
```

```python
import functools
import math

import jax
import jax.numpy as jnp
from jax import lax
from jax.experimental import pallas as pl
from jax.experimental.pallas import tpu as pltpu
from jax.sharding import PartitionSpec as P

F32 = jnp.float32
BF16 = jnp.bfloat16
GROUP = 8
DEPTH = 24
SPARE = 21
CENTER = 0.5


def pieces(value):
    high = value.astype(BF16).astype(F32)
    rest = value - high
    middle = rest.astype(BF16).astype(F32)
    low = (rest - middle).astype(BF16).astype(F32)
    return high, middle, low


def pieces_outside(value):
    high = lax.reduce_precision(value, 8, 7)
    rest = value - high
    middle = lax.reduce_precision(rest, 8, 7)
    low = lax.reduce_precision(rest - middle, 8, 7)
    return high, middle, low


LEFT = (0, 0, 1, 1, 0, 2)
RIGHT = (0, 1, 0, 1, 2, 0)


def cell_features(xy):
    x, y = xy[0] - CENTER, xy[1] - CENTER
    px, py, pn = pieces_outside(x), pieces_outside(y), pieces_outside(x * x + y * y)
    one, zero = jnp.ones_like(x), jnp.zeros_like(x)
    columns = [px[i] for i in LEFT] + [py[i] for i in LEFT] + [pn[i] for i in LEFT]
    columns += [one] * 3 + [zero] * (DEPTH - SPARE)
    return jnp.stack(columns, axis=1).astype(BF16)


def point_features(points_ref, length_ref, extra, table_ref):
    length = length_ref[...]
    scale = 0.5 / (length * length)
    x = points_ref[0] - CENTER
    y = points_ref[1] - CENTER
    px = pieces(x * (2.0 * scale))
    py = pieces(y * (2.0 * scale))
    ps = pieces(jnp.broadcast_to(-scale, x.shape))
    pn = pieces((x * x + y * y) * -scale)
    rows = [px[i] for i in RIGHT] + [py[i] for i in RIGHT] + [ps[i] for i in RIGHT]
    rows += list(pn) + [extra] + [jnp.zeros_like(x)] * (DEPTH - SPARE - 1)
    for place, row in enumerate(rows):
        for lane in range(GROUP):
            table_ref[lane, place : place + 1, :] = row[lane : lane + 1, :]


def forward_body(tile, feat_ref, points_ref, weight_ref, length_ref, height_ref, out_ref, table_ref, wide_ref):
    point_features(points_ref, length_ref, weight_ref[...], table_ref)
    feat = feat_ref[...]
    count = weight_ref.shape[1]

    def one(j, carry):
        total = jnp.zeros((feat.shape[0], 128), F32)
        for start in range(0, count, tile):
            part = table_ref[j, :, start : start + tile].astype(BF16)
            value = jnp.exp(jnp.dot(feat, part, preferred_element_type=F32))
            for lane in range(0, tile, 128):
                w = table_ref[j, SPARE : SPARE + 1, start + lane : start + lane + 128]
                total = total + value[:, lane : lane + 128] * w
        wide_ref[j] = total
        return carry

    lax.fori_loop(0, GROUP, one, 0)
    for j in range(GROUP):
        total = jnp.sum(wide_ref[j].T, axis=0, keepdims=True)
        out_ref[j : j + 1, :] = total * height_ref[j : j + 1, :]


def backward_body(
    tile, feat_ref, points_ref, grad_ref, length_ref, height_ref, out_ref, table_ref, wide_ref, sum_ref
):
    count = points_ref.shape[2]
    point_features(points_ref, length_ref, jnp.zeros((GROUP, count), F32), table_ref)
    feat = feat_ref[...]
    rows = feat.shape[0]
    grad = (grad_ref[...] * height_ref[...]).T
    for j in range(GROUP):
        wide_ref[j] = jnp.broadcast_to(grad[:, j : j + 1], (rows, 128))

    def one(j, carry):
        for start in range(0, count, tile):
            part = table_ref[j, :, start : start + tile].astype(BF16)
            value = jnp.exp(jnp.dot(feat, part, preferred_element_type=F32))
            for lane in range(0, tile, 128):
                term = value[:, lane : lane + 128] * wide_ref[j]
                sum_ref[j, :, start + lane : start + lane + 128] = jnp.sum(
                    term.reshape(rows // 8, 8, 128), axis=0
                )
        return carry

    lax.fori_loop(0, GROUP, one, 0)
    for j in range(GROUP):
        out_ref[j : j + 1, :] = jnp.sum(sum_ref[j], axis=0, keepdims=True)


def middle_body(scale, index_ref, expr_ref, latent_ref, mixing_ref, noise_ref, mix_out_ref, cell_out_ref):
    rows = index_ref.shape[0]
    table = expr_ref.shape[0]
    pick = (lax.broadcasted_iota(jnp.int32, (rows, table), 1) == index_ref[...]).astype(F32).astype(BF16)
    observed = jnp.dot(pick, expr_ref[...], preferred_element_type=F32)
    latent = latent_ref[...]
    mixing = mixing_ref[...]
    predicted = lax.dot_general(latent, mixing, (((0,), (0,)), ((), ())), preferred_element_type=F32)
    weighted = (noise_ref[...] * (observed - predicted)).astype(BF16)
    mix_out_ref[...] = scale * jnp.dot(latent, weighted, preferred_element_type=F32)

    @pl.when(pl.program_id(0) == 0)
    def _():
        cell_out_ref[...] = jnp.zeros_like(cell_out_ref)

    cell_out_ref[...] += scale * lax.dot_general(
        mixing, weighted, (((1,), (1,)), ((), ())), preferred_element_type=F32
    )


def products(body, out_shape, scratch, feat, points, other, length, height):
    lats, count = points.shape[1], points.shape[2]
    rows = feat.shape[0]
    tile = min(256, count)
    work = rows * lats * count
    return pl.pallas_call(
        functools.partial(body, tile),
        grid=(lats // GROUP,),
        in_specs=[
            pl.BlockSpec((rows, DEPTH), lambda i: (0, 0)),
            pl.BlockSpec((2, GROUP, count), lambda i: (0, i, 0)),
            pl.BlockSpec((GROUP, other.shape[1]), lambda i: (i, 0)),
            pl.BlockSpec((GROUP, 1), lambda i: (i, 0)),
            pl.BlockSpec((GROUP, 1), lambda i: (i, 0)),
        ],
        out_specs=pl.BlockSpec((GROUP, out_shape[1]), lambda i: (i, 0)),
        out_shape=jax.ShapeDtypeStruct(out_shape, F32),
        scratch_shapes=[pltpu.VMEM((GROUP, DEPTH, count), F32), *scratch],
        cost_estimate=pl.CostEstimate(
            flops=2 * DEPTH * work, transcendentals=work, bytes_accessed=12 * lats * count
        ),
        compiler_params=pltpu.CompilerParams(vmem_limit_bytes=40 * 2**20),
    )(feat, points, other, length[:, None], height[:, None])


def middle(scale, cell_index, expr_table, latent, mixing, noise_prec):
    rows = cell_index.shape[0]
    table, genes = expr_table.shape
    lats = latent.shape[0]
    tile = min(512, genes)
    return pl.pallas_call(
        functools.partial(middle_body, scale),
        grid=(genes // tile,),
        in_specs=[
            pl.BlockSpec((rows, 1), lambda i: (0, 0)),
            pl.BlockSpec((table, tile), lambda i: (0, i)),
            pl.BlockSpec((lats, rows), lambda i: (0, 0)),
            pl.BlockSpec((lats, tile), lambda i: (0, i)),
            pl.BlockSpec((1, tile), lambda i: (0, i)),
        ],
        out_specs=[
            pl.BlockSpec((lats, tile), lambda i: (0, i)),
            pl.BlockSpec((lats, rows), lambda i: (0, 0)),
        ],
        out_shape=[
            jax.ShapeDtypeStruct((lats, genes), F32),
            jax.ShapeDtypeStruct((lats, rows), F32),
        ],
        compiler_params=pltpu.CompilerParams(vmem_limit_bytes=40 * 2**20),
    )(cell_index[:, None], expr_table, latent, mixing, noise_prec[None, :])


def on_device(
    cell_index,
    coords_table,
    expr_table,
    inducing,
    ind_weights,
    lengthscale,
    variance,
    mixing,
    noise_prec,
):
    gene_count = lax.axis_size("gene")
    lat_count = lax.axis_size("lat")
    sub_count = lax.axis_size("sub")
    bat_rows = cell_index.shape[0]
    per_block = bat_rows // gene_count
    block_count = lat_count * sub_count
    gene_place = lax.axis_index("gene")
    mine = lax.dynamic_slice_in_dim(cell_index, gene_place * per_block, per_block, 0)
    picks = mine[:, None] == jnp.arange(coords_table.shape[1], dtype=mine.dtype)[None, :]
    local_xy = jnp.sum(jnp.where(picks[None], coords_table[:, None, :], 0.0), axis=2)
    kernel_xy = lax.all_gather(local_xy, ("lat", "sub"), axis=1, tiled=True)
    feat = cell_features(kernel_xy)
    rows = feat.shape[0]
    lats, count = ind_weights.shape
    local_latent = products(
        forward_body, (lats, rows), [pltpu.VMEM((GROUP, rows, 128), F32)], feat, inducing, ind_weights, lengthscale, variance
    )
    swapped = lax.all_to_all(local_latent, "lat", split_axis=1, concat_axis=0, tiled=True)
    summed = lax.psum_scatter(swapped, "sub", scatter_dimension=1, tiled=True).astype(BF16)
    latent = lax.all_gather(summed, "gene", axis=1, tiled=True)
    grad_scale = -1.0 / math.sqrt(bat_rows * block_count)
    mixing_term, cell_term = middle(grad_scale, cell_index, expr_table, latent, mixing, noise_prec)
    grad_mixing = lax.psum(mixing_term, ("lat", "sub"))
    shared = lax.psum_scatter(cell_term, "gene", scatter_dimension=1, tiled=True)
    paired = lax.all_gather(shared, "sub", axis=1, tiled=True)
    latent_grad = lax.all_to_all(paired, "lat", split_axis=0, concat_axis=1, tiled=True)
    scratch = [pltpu.VMEM((GROUP, rows, 128), F32), pltpu.VMEM((GROUP, 8, count), F32)]
    partial_inducing = products(
        backward_body, (lats, count), scratch, feat, inducing, latent_grad, lengthscale, variance
    )
    grad_inducing = lax.psum(partial_inducing, "gene")
    return (grad_mixing, grad_inducing)


def solution(mesh):
    in_specs = (
        P(("group", "lat", "sub")),
        P("group", ("lat", "sub")),
        P(("group", "lat", "sub"), "gene"),
        P("group", "lat", "sub"),
        P(("group", "lat"), "sub"),
        P(("group", "lat")),
        P(("group", "lat")),
        P("group", "gene"),
        P(("group", "gene")),
    )
    out_specs = (P("group", "gene"), P(("group", "lat"), "sub"))
    return jax.shard_map(
        on_device, mesh=mesh, in_specs=in_specs, out_specs=out_specs, check_vma=False
    )
```

```python
import functools
import math

import jax
import jax.numpy as jnp
from jax import lax
from jax.experimental import pallas as pl
from jax.experimental.pallas import tpu as pltpu
from jax.sharding import PartitionSpec as P

F32 = jnp.float32
BF16 = jnp.bfloat16
GROUP = 8
DEPTH = 24
SPARE = 21
CENTER = 0.5


def pieces(value):
    high = value.astype(BF16).astype(F32)
    rest = value - high
    middle = rest.astype(BF16).astype(F32)
    low = (rest - middle).astype(BF16).astype(F32)
    return high, middle, low


def pieces_outside(value):
    high = lax.reduce_precision(value, 8, 7)
    rest = value - high
    middle = lax.reduce_precision(rest, 8, 7)
    low = lax.reduce_precision(rest - middle, 8, 7)
    return high, middle, low


LEFT = (0, 0, 1, 1, 0, 2)
RIGHT = (0, 1, 0, 1, 2, 0)


def cell_features(xy):
    x, y = xy[0] - CENTER, xy[1] - CENTER
    px, py, pn = pieces_outside(x), pieces_outside(y), pieces_outside(x * x + y * y)
    one, zero = jnp.ones_like(x), jnp.zeros_like(x)
    columns = [px[i] for i in LEFT] + [py[i] for i in LEFT] + [pn[i] for i in LEFT]
    columns += [one] * 3 + [zero] * (DEPTH - SPARE)
    return jnp.stack(columns, axis=1).astype(BF16)


def point_features(points_ref, length_ref, extra, table_ref):
    length = length_ref[...]
    scale = 0.5 / (length * length)
    x = points_ref[0] - CENTER
    y = points_ref[1] - CENTER
    px = pieces(x * (2.0 * scale))
    py = pieces(y * (2.0 * scale))
    ps = pieces(jnp.broadcast_to(-scale, x.shape))
    pn = pieces((x * x + y * y) * -scale)
    rows = [px[i] for i in RIGHT] + [py[i] for i in RIGHT] + [ps[i] for i in RIGHT]
    rows += list(pn) + [extra] + [jnp.zeros_like(x)] * (DEPTH - SPARE - 1)
    for place, row in enumerate(rows):
        for lane in range(GROUP):
            table_ref[lane, place : place + 1, :] = row[lane : lane + 1, :]


def forward_body(tile, feat_ref, points_ref, weight_ref, length_ref, height_ref, out_ref, table_ref, wide_ref):
    point_features(points_ref, length_ref, weight_ref[...], table_ref)
    feat = feat_ref[...]
    count = weight_ref.shape[1]

    def one(j, carry):
        total = jnp.zeros((feat.shape[0], 128), F32)
        for start in range(0, count, tile):
            part = table_ref[j, :, start : start + tile].astype(BF16)
            value = jnp.exp(jnp.dot(feat, part, preferred_element_type=F32))
            for lane in range(0, tile, 128):
                w = table_ref[j, SPARE : SPARE + 1, start + lane : start + lane + 128]
                total = total + value[:, lane : lane + 128] * w
        wide_ref[j] = total
        return carry

    lax.fori_loop(0, GROUP, one, 0)
    for j in range(GROUP):
        total = jnp.sum(wide_ref[j].T, axis=0, keepdims=True)
        total = total * height_ref[j : j + 1, :]
        blocks, _, width = out_ref.shape
        for block in range(blocks):
            out_ref[block, j : j + 1, :] = total[:, block * width : (block + 1) * width]


def backward_body(
    tile, feat_ref, points_ref, grad_ref, length_ref, height_ref, out_ref, table_ref, wide_ref, sum_ref
):
    count = points_ref.shape[2]
    point_features(points_ref, length_ref, jnp.zeros((GROUP, count), F32), table_ref)
    feat = feat_ref[...]
    rows = feat.shape[0]
    grad = (grad_ref[...] * height_ref[...]).T
    for j in range(GROUP):
        wide_ref[j] = jnp.broadcast_to(grad[:, j : j + 1], (rows, 128))

    def one(j, carry):
        for start in range(0, count, tile):
            part = table_ref[j, :, start : start + tile].astype(BF16)
            value = jnp.exp(jnp.dot(feat, part, preferred_element_type=F32))
            for lane in range(0, tile, 128):
                term = value[:, lane : lane + 128] * wide_ref[j]
                sum_ref[j, :, start + lane : start + lane + 128] = jnp.sum(
                    term.reshape(rows // 8, 8, 128), axis=0
                )
        return carry

    lax.fori_loop(0, GROUP, one, 0)
    for j in range(GROUP):
        out_ref[j : j + 1, :] = jnp.sum(sum_ref[j], axis=0, keepdims=True)


def middle_body(scale, index_ref, expr_ref, latent_ref, mixing_ref, noise_ref, mix_out_ref, chunk_ref, cell_ref):
    rows = index_ref.shape[0]
    table = expr_ref.shape[0]
    pick = (lax.broadcasted_iota(jnp.int32, (rows, table), 1) == index_ref[...]).astype(F32).astype(BF16)
    observed = jnp.dot(pick, expr_ref[...], preferred_element_type=F32)
    latent = latent_ref[...]
    mixing = mixing_ref[...]
    predicted = lax.dot_general(latent, mixing, (((0,), (0,)), ((), ())), preferred_element_type=F32)
    weighted = (noise_ref[...] * (observed - predicted)).astype(BF16)
    mix_out_ref[...] = scale * jnp.dot(latent, weighted, preferred_element_type=F32)

    @pl.when(pl.program_id(0) == 0)
    def _():
        cell_ref[...] = jnp.zeros_like(cell_ref)

    cell_ref[...] += scale * lax.dot_general(
        mixing, weighted, (((1,), (1,)), ((), ())), preferred_element_type=F32
    )

    @pl.when(pl.program_id(0) == pl.num_programs(0) - 1)
    def _():
        genes, lats, depth, width = chunk_ref.shape
        for gene in range(genes):
            for lat in range(lats):
                chunk_ref[gene, lat] = cell_ref[
                    lat * depth : (lat + 1) * depth, gene * width : (gene + 1) * width
                ]


AXES = ("gene", "lat", "sub")


def place_of(rank, sizes):
    return rank // (sizes[1] * sizes[2]), rank // sizes[2] % sizes[1], rank % sizes[2]


def greet(ranks):
    barrier = pltpu.get_barrier_semaphore()
    for device in ranks:
        pl.semaphore_signal(barrier, inc=1, device_id=device, device_id_type=pl.DeviceIdType.MESH)
    pl.semaphore_wait(barrier, len(ranks))


def exchange_body(sizes, chunk_of, finish, send_ref, out_ref, recv_ref, send_sem, recv_sem, own_sem):
    total = sizes[0] * sizes[1] * sizes[2]
    place = tuple(lax.axis_index(axis) for axis in AXES)
    me = (place[0] * sizes[1] + place[1]) * sizes[2] + place[2]
    peers = [place_of(lax.rem(me + k, total), sizes) for k in range(1, total)]
    greet([dict(zip(AXES, peer)) for peer in peers])
    copies = []
    for k, peer in enumerate(peers):
        copy = pltpu.make_async_remote_copy(
            src_ref=send_ref.at[chunk_of(peer)],
            dst_ref=recv_ref.at[me],
            send_sem=send_sem.at[k],
            recv_sem=recv_sem.at[k],
            device_id=dict(zip(AXES, peer)),
            device_id_type=pl.DeviceIdType.MESH,
        )
        copy.start()
        copies.append(copy)
    own = pltpu.make_async_copy(send_ref.at[chunk_of(place)], recv_ref.at[me], own_sem)
    own.start()
    own.wait()
    for copy in copies:
        copy.wait()
    finish(recv_ref, out_ref)


def exchange(sizes, chunk_of, finish, out, collective_id, send):
    total = sizes[0] * sizes[1] * sizes[2]
    return pl.pallas_call(
        functools.partial(exchange_body, sizes, chunk_of, finish),
        in_specs=[pl.BlockSpec(memory_space=pltpu.VMEM)],
        out_specs=pl.BlockSpec(memory_space=pltpu.VMEM),
        out_shape=out,
        scratch_shapes=[
            pltpu.VMEM((total, *send.shape[1:]), F32),
            pltpu.SemaphoreType.DMA((total - 1,)),
            pltpu.SemaphoreType.DMA((total - 1,)),
            pltpu.SemaphoreType.DMA,
        ],
        compiler_params=pltpu.CompilerParams(collective_id=collective_id, has_side_effects=True),
    )(send)


def gene_sum_body(genes, x_ref, out_ref, recv_ref, sum_ref, all_ref, send_sem, recv_sem, back_sem, full_sem):
    me = lax.axis_index("gene")
    width = sum_ref.shape[1]
    peers = [lax.rem(me + k, genes) for k in range(1, genes)]
    greet([{"gene": peer} for peer in peers])

    def columns(place):
        return pl.ds(pl.multiple_of(place * width, 128), width)

    copies = []
    for k, peer in enumerate(peers):
        copy = pltpu.make_async_remote_copy(
            src_ref=x_ref.at[:, columns(peer)],
            dst_ref=recv_ref.at[k],
            send_sem=send_sem.at[k],
            recv_sem=recv_sem.at[k],
            device_id={"gene": peer},
            device_id_type=pl.DeviceIdType.MESH,
        )
        copy.start()
        copies.append(copy)
    for copy in copies:
        copy.wait()
    value = x_ref[:, columns(me)]
    for k in range(genes - 1):
        value = value + recv_ref[k]
    sum_ref[...] = value
    backs = []
    for k, peer in enumerate(peers):
        copy = pltpu.make_async_remote_copy(
            src_ref=sum_ref,
            dst_ref=all_ref.at[k],
            send_sem=back_sem.at[k],
            recv_sem=full_sem.at[k],
            device_id={"gene": peer},
            device_id_type=pl.DeviceIdType.MESH,
        )
        copy.start()
        backs.append(copy)
    out_ref[:, columns(me)] = value
    for k, copy in enumerate(backs):
        copy.wait()
        out_ref[:, columns(lax.rem(me + genes - 1 - k, genes))] = all_ref[k]


def gene_sum(genes, collective_id, x):
    rows, count = x.shape
    width = count // genes
    sems = pltpu.SemaphoreType.DMA((genes - 1,))
    return pl.pallas_call(
        functools.partial(gene_sum_body, genes),
        in_specs=[pl.BlockSpec(memory_space=pltpu.VMEM)],
        out_specs=pl.BlockSpec(memory_space=pltpu.VMEM),
        out_shape=jax.ShapeDtypeStruct(x.shape, F32),
        scratch_shapes=[
            pltpu.VMEM((genes - 1, rows, width), F32),
            pltpu.VMEM((rows, width), F32),
            pltpu.VMEM((genes - 1, rows, width), F32),
            sems,
            sems,
            sems,
            sems,
        ],
        compiler_params=pltpu.CompilerParams(
            collective_id=collective_id, has_side_effects=True, vmem_limit_bytes=40 * 2**20
        ),
    )(x)


def products(body, out_shape, scratch, feat, points, other, length, height):
    lats, count = points.shape[1], points.shape[2]
    rows = feat.shape[0]
    tile = min(256, count)
    work = rows * lats * count
    return pl.pallas_call(
        functools.partial(body, tile),
        grid=(lats // GROUP,),
        in_specs=[
            pl.BlockSpec((rows, DEPTH), lambda i: (0, 0)),
            pl.BlockSpec((2, GROUP, count), lambda i: (0, i, 0)),
            pl.BlockSpec((GROUP, other.shape[1]), lambda i: (i, 0)),
            pl.BlockSpec((GROUP, 1), lambda i: (i, 0)),
            pl.BlockSpec((GROUP, 1), lambda i: (i, 0)),
        ],
        out_specs=pl.BlockSpec(
            (*out_shape[:-2], GROUP, out_shape[-1]), lambda i: (*(0 for _ in out_shape[2:]), i, 0)
        ),
        out_shape=jax.ShapeDtypeStruct(out_shape, F32),
        scratch_shapes=[pltpu.VMEM((GROUP, DEPTH, count), F32), *scratch],
        cost_estimate=pl.CostEstimate(
            flops=2 * DEPTH * work, transcendentals=work, bytes_accessed=12 * lats * count
        ),
        compiler_params=pltpu.CompilerParams(vmem_limit_bytes=40 * 2**20),
    )(feat, points, other, length[:, None], height[:, None])


def middle(scale, chunks, cell_index, expr_table, latent, mixing, noise_prec):
    rows = cell_index.shape[0]
    table, genes = expr_table.shape
    lats = latent.shape[0]
    tile = min(512, genes)
    return pl.pallas_call(
        functools.partial(middle_body, scale),
        grid=(genes // tile,),
        in_specs=[
            pl.BlockSpec((rows, 1), lambda i: (0, 0)),
            pl.BlockSpec((table, tile), lambda i: (0, i)),
            pl.BlockSpec((lats, rows), lambda i: (0, 0)),
            pl.BlockSpec((lats, tile), lambda i: (0, i)),
            pl.BlockSpec((1, tile), lambda i: (0, i)),
        ],
        out_specs=[
            pl.BlockSpec((lats, tile), lambda i: (0, i)),
            pl.BlockSpec(chunks, lambda i: (0, 0, 0, 0)),
        ],
        out_shape=[
            jax.ShapeDtypeStruct((lats, genes), F32),
            jax.ShapeDtypeStruct(chunks, F32),
        ],
        scratch_shapes=[pltpu.VMEM((lats, rows), F32)],
        compiler_params=pltpu.CompilerParams(vmem_limit_bytes=40 * 2**20),
    )(cell_index[:, None], expr_table, latent, mixing, noise_prec[None, :])


def on_device(
    cell_index,
    coords_table,
    expr_table,
    inducing,
    ind_weights,
    lengthscale,
    variance,
    mixing,
    noise_prec,
):
    gene_count = lax.axis_size("gene")
    lat_count = lax.axis_size("lat")
    sub_count = lax.axis_size("sub")
    bat_rows = cell_index.shape[0]
    per_block = bat_rows // gene_count
    block_count = lat_count * sub_count
    gene_place = lax.axis_index("gene")
    mine = lax.dynamic_slice_in_dim(cell_index, gene_place * per_block, per_block, 0)
    picks = mine[:, None] == jnp.arange(coords_table.shape[1], dtype=mine.dtype)[None, :]
    local_xy = jnp.sum(jnp.where(picks[None], coords_table[:, None, :], 0.0), axis=2)
    kernel_xy = lax.all_gather(local_xy, ("lat", "sub"), axis=1, tiled=True)
    feat = cell_features(kernel_xy)
    rows = feat.shape[0]
    lats, count = ind_weights.shape
    local_latent = products(
        forward_body, (block_count, lats, per_block), [pltpu.VMEM((GROUP, rows, 128), F32)], feat, inducing, ind_weights, lengthscale, variance
    )
    sizes = (gene_count, lat_count, sub_count)

    def finish_latent(recv_ref, out_ref):
        for gene in range(gene_count):
            for lat in range(lat_count):
                first = (gene * lat_count + lat) * sub_count
                value = recv_ref[first]
                for sub in range(1, sub_count):
                    value = value + recv_ref[first + sub]
                out_ref[lat * lats : (lat + 1) * lats, gene * per_block : (gene + 1) * per_block] = value

    def finish_grad(recv_ref, out_ref):
        for block in range(block_count):
            value = recv_ref[block]
            for gene in range(1, gene_count):
                value = value + recv_ref[gene * block_count + block]
            out_ref[:, block * per_block : (block + 1) * per_block] = value

    latent = exchange(
        sizes,
        lambda peer: peer[1] * sub_count + peer[2],
        finish_latent,
        jax.ShapeDtypeStruct((lat_count * lats, bat_rows), F32),
        0,
        local_latent,
    ).astype(BF16)
    grad_scale = -1.0 / math.sqrt(bat_rows * block_count)
    chunks = (gene_count, lat_count, lats, per_block)
    mixing_term, cell_term = middle(grad_scale, chunks, cell_index, expr_table, latent, mixing, noise_prec)
    grad_mixing = lax.psum(mixing_term, ("lat", "sub"))
    latent_grad = exchange(
        sizes,
        lambda peer: peer[0] * lat_count + peer[1],
        finish_grad,
        jax.ShapeDtypeStruct((lats, rows), F32),
        1,
        cell_term.reshape(gene_count * lat_count, lats, per_block),
    )
    scratch = [pltpu.VMEM((GROUP, rows, 128), F32), pltpu.VMEM((GROUP, 8, count), F32)]
    partial_inducing = products(
        backward_body, (lats, count), scratch, feat, inducing, latent_grad, lengthscale, variance
    )
    grad_inducing = gene_sum(gene_count, 2, partial_inducing)
    return (grad_mixing, grad_inducing)


def solution(mesh):
    in_specs = (
        P(("group", "lat", "sub")),
        P("group", ("lat", "sub")),
        P(("group", "lat", "sub"), "gene"),
        P("group", "lat", "sub"),
        P(("group", "lat"), "sub"),
        P(("group", "lat")),
        P(("group", "lat")),
        P("group", "gene"),
        P(("group", "gene")),
    )
    out_specs = (P("group", "gene"), P(("group", "lat"), "sub"))
    return jax.shard_map(
        on_device, mesh=mesh, in_specs=in_specs, out_specs=out_specs, check_vma=False
    )
```
